128 devices in a mesh: row: 8 (over z, x_hi), col: 16 (over x_lo, y, core).
Axes of the slice: x: 4 (x_hi: 2, x_lo: 2; x = x_hi * 2 + x_lo), y: 4, z: 4, core: 2. Of those that a mesh axis runs over, the one named last changes fastest.
Arguments:
- downdates: float32 [16384, 16384], P('row', 'col'), may hold values from -4 to 4
- centers: float32 [440, 16384], P(None, ('row', 'col')), may hold values from -6 to 6
- diag_inverse: float32 [1024, 1024], P('col'), as said below
- block_map: int32 [16], replicated, may hold values from 0 to 15, each once
- panel_index: int32 [1], replicated, may hold values from 0 to 7
Outputs:
- panel_factor: float32 [16384, 1024], P(('row', 'col'))
- remaining: float32 [16384, 16384], P('row', 'col')
The draws below stay inside these ranges and needn't reach their ends.
Inputs may be any that keep to these rules, and one draw needn't show every extreme that they name: diag_inverse is lower triangular with a positive diagonal.
All inputs are finite; a program needn't handle non-finite values.
Results may differ from the reference program's by a relative error of at most 0.0003.
Values sent between devices are 32-bit elements; how exact they have to be, the bound alone decides.
A program may use at most 128 MiB of HBM per device.

```python
import jax
import jax.numpy as jnp
from jax import lax

ORDER = 16384
PANEL = 1024
FEAT = 440
BLOCKS = 16


def draw_diag_inverse(key, part):
    lower_key = jax.random.fold_in(key, 11)
    diag_key = jax.random.fold_in(key, 23)
    lower_part = jax.random.normal(lower_key, (PANEL, PANEL), jnp.float32) * (2.0 / PANEL)
    diag_part = jnp.exp(jax.random.uniform(diag_key, (PANEL,), jnp.float32, 0.0, jnp.log(3.0))) / jnp.sqrt(1.0 * PANEL)
    row_ids = jnp.arange(PANEL)[:, None]
    col_ids = jnp.arange(PANEL)[None, :]
    result = jnp.where(row_ids > col_ids, lower_part, 0.0) + jnp.where(row_ids == col_ids, diag_part[:, None], 0.0)
    return result.astype(jnp.float32)


def level_of(stream_key, dims, split, low, high):
    def one(dim, shards_of):
        heights = jax.random.uniform(jax.random.fold_in(jax.random.fold_in(stream_key, 6), dim), (shards_of,), jnp.float32, low / len(split), high / len(split))
        return jnp.repeat(jnp.exp(heights), dims[dim] // shards_of).reshape((-1,) + (1,) * (len(dims) - dim - 1))

    gain = one(*split[0])
    for cut in split[1:]:
        gain = gain * one(*cut)
    return gain


def gaussian(own_key, extent, deviation, limit, split=(), kind=jnp.bfloat16):
    drawn = deviation * jax.random.normal(own_key, extent, jnp.float32)
    if split:
        drawn = drawn * level_of(own_key, extent, split, -0.22, 0.18)
    return jnp.clip(drawn, -limit, limit).astype(kind)


def setup_inputs(seed: int = 0) -> dict:
    seeds = jax.random.split(jax.random.key(seed), 6)
    downdates = gaussian(seeds[0], (ORDER, ORDER), 0.3, 4.0, ((0, 8), (1, 16)), jnp.float32)
    centers = gaussian(seeds[1], (FEAT, ORDER), 1.0, 6.0, ((1, 128),), jnp.float32)
    diag_inverse = draw_diag_inverse(jax.random.fold_in(seeds[5], 71), 0)
    block_map = jax.random.permutation(seeds[3], BLOCKS).astype(jnp.int32)
    panel_index = jax.random.randint(seeds[4], (1,), 0, BLOCKS // 2).astype(jnp.int32)
    return dict(downdates=downdates, centers=centers, diag_inverse=diag_inverse, block_map=block_map, panel_index=panel_index)


highest = lax.Precision.HIGHEST


def kernel_tile(left_side, right_side):
    left_norm = jnp.sum(left_side * left_side, axis=0)
    right_norm = jnp.sum(right_side * right_side, axis=0)
    cross_term = lax.dot_general(left_side, right_side, (((0,), (0,)), ((), ())), precision=highest, preferred_element_type=jnp.float32)
    return jnp.exp(-(0.5 / FEAT) * (left_norm[:, None] + right_norm[None, :] - 2.0 * cross_term))


def reference(downdates, centers, diag_inverse, block_map, panel_index):
    panel_number = panel_index[0]
    block_ids = jnp.arange(BLOCKS, dtype=jnp.int32)
    panel_block = jnp.sum(block_ids * (block_map == panel_number).astype(jnp.int32)).astype(jnp.int32)
    panel_start = (panel_block * PANEL).astype(jnp.int32)
    panel_centers = lax.dynamic_slice_in_dim(centers, panel_start, PANEL, 1)
    raw_panel = kernel_tile(centers, panel_centers) + lax.dynamic_slice_in_dim(downdates, panel_start, PANEL, 1)
    row_alive = jnp.repeat(block_map > panel_number, PANEL)
    product = lax.dot_general(raw_panel, diag_inverse, (((1,), (1,)), ((), ())), precision=highest, preferred_element_type=jnp.float32)
    factor = jnp.where(row_alive[:, None], product, 0.0)

    def one_block(block_index):
        row_begin = (block_index * PANEL).astype(jnp.int32)
        block_centers = lax.dynamic_slice_in_dim(centers, row_begin, PANEL, 1)
        block_rows = lax.dynamic_slice_in_dim(downdates, row_begin, PANEL, 0)
        block_factor = lax.dynamic_slice_in_dim(factor, row_begin, PANEL, 0)
        update = lax.dot_general(block_factor, factor, (((1,), (1,)), ((), ())), precision=highest, preferred_element_type=jnp.float32)
        return kernel_tile(block_centers, centers) + block_rows - update

    remaining = lax.map(one_block, block_ids).reshape(ORDER, ORDER)
    return factor, remaining
```

```python
import functools

import jax
import jax.numpy as jnp
from jax import lax
from jax.experimental import pallas as pl
from jax.experimental.pallas import tpu as pltpu
from jax.sharding import PartitionSpec as P

PANEL = 1024
FEAT = 440
KPAD = 512
BLOCKS = 16
MESH = pl.DeviceIdType.MESH
F32 = jnp.float32
BF16 = jnp.bfloat16
CHUNKS = 16
LAG = 4


def place():
    row = lax.axis_index("row")
    col = lax.axis_index("col")
    return dict(z=row // 2, xh=row % 2, xl=col // 8, y=(col // 2) % 4, a=col % 2)


def device(p, **changes):
    q = dict(p)
    q.update(changes)
    return (q["z"] * 2 + q["xh"], q["xl"] * 8 + q["y"] * 2 + q["a"])


def neighbours(p):
    return dict(
        yp=device(p, y=(p["y"] + 1) % 4),
        ym=device(p, y=(p["y"] + 3) % 4),
        xp=device(p, xl=1 - p["xl"]),
        zp=device(p, z=(p["z"] + 1) % 4),
        zm=device(p, z=(p["z"] + 3) % 4),
        xx=device(p, xh=1 - p["xh"]),
        co=device(p, a=1 - p["a"]),
    )


def entry_barrier(near):
    barrier = pltpu.get_barrier_semaphore()
    for where in near.values():
        pl.semaphore_signal(barrier, inc=1, device_id=where, device_id_type=MESH)
    pl.semaphore_wait(barrier, len(near))


def remote(src, dst, send, recv, where):
    return pltpu.make_async_remote_copy(
        src_ref=src, dst_ref=dst, send_sem=send, recv_sem=recv, device_id=where, device_id_type=MESH
    )


def branch_flags(first_ring, d, m, part):
    rel = (d - m + 16) % 4
    if part == 0:
        up = (first_ring & (d != 3)) | (~first_ring & (rel <= 1))
        down = ~first_ring & (rel == 0)
    else:
        up = ~first_ring & (rel == 0)
        down = (first_ring & (d != 1)) | (~first_ring & ((rel == 0) | (rel == 3)))
    across = first_ring & (rel == 0)
    return up, down, across


def column_state(p):
    k = p["xl"] * 4 + p["y"]
    d = (p["z"] - k // 2 + 4) % 4
    first = p["xh"] == k % 2
    diagonal = (p["z"] * 2 + p["xh"]) == k
    return d, first, diagonal


def gather_kernel(x_ref, l_ref, d_ref, xg, li, dx, own, rx, rl, rk, rc, sx, sl, sk, sc, sd):
    p = place()
    near = neighbours(p)
    a, y, xl = p["a"], p["y"], p["xl"]
    d, first, diagonal = column_state(p)
    entry_barrier(near)

    def slot(xl_, y_, a_):
        return xl_ * 8 + y_ * 2 + a_

    def at(table, s):
        return xg.at[s // 8, s % 8] if table == 0 else li.at[s]

    started = []

    def send(table, s, way, src=None):
        src = at(table, s) if src is None else src
        sems, recv = (sx, rx) if table == 0 else (sl, rl)
        way_index = ("yp", "ym", "xp", "co").index(way)
        copy = remote(src, at(table, s), sems.at[way_index, s], recv.at[s], near[way])
        copy.start()
        started.append(copy)

    def arrived(table, s):
        recv = rx if table == 0 else rl
        copy = pltpu.make_async_copy(at(table, s), at(table, s), recv.at[s])
        copy.wait()

    mine = slot(xl, y, a)
    before, after, far = (y + 3) % 4, (y + 1) % 4, (y + 2) % 4

    def first_sends(table):
        src = x_ref if table == 0 else l_ref
        for way in ("yp", "ym", "xp", "co"):
            send(table, mine, way, src)
        keep = pltpu.make_async_copy(src, at(table, mine), own.at[table])
        keep.start()
        return keep

    keep_x = first_sends(0)
    keep_l = first_sends(1)
    half = PANEL
    swap = remote(d_ref.at[pl.ds((1 - a) * half, half)], dx, sd.at[0], sd.at[1], near["co"])
    swap.start()

    def row_steps(table):
        steps = []

        def step(s, *ways):
            def run():
                arrived(table, s)
                for way in ways:
                    send(table, s, way)

            steps.append(run)

        step(slot(1 - xl, y, a), "yp", "ym", "co")
        if table == 0:
            step(slot(xl, before, a), "yp", "co")
            step(slot(xl, after, a), "co")
        else:
            step(slot(xl, after, a), "ym", "co")
            step(slot(xl, before, a), "co")
        step(slot(1 - xl, before, a), "co")
        step(slot(1 - xl, after, a), "co")
        step(slot(xl, far, a), "xp", "co")
        step(slot(1 - xl, far, a), "co")
        return steps

    for run in row_steps(0):
        run()
    for xs in range(2):
        for ys in range(4):
            arrived(0, slot(xs, ys, 1 - a))
    keep_x.wait()

    def column_copies(m, part, src, is_first, dist):
        up, down, across = branch_flags(is_first, dist, m, part)
        j = 2 * m + part
        dst = xg.at[2 + a, j]
        out = []
        for index, (flag, way) in enumerate(((up, "zp"), (down, "zm"), (across, "xx"))):
            out.append((flag, remote(src, dst, sk.at[index, j], rk.at[j], near[way])))
        return out

    true = d >= 0

    @pl.when(diagonal)
    def _():
        for m in range(4):
            for part in range(2):
                for flag, copy in column_copies(m, part, xg.at[a, 2 * m + part], true, 0 * d):
                    @pl.when(flag)
                    def _():
                        copy.start()

    def column_step(m):
        @pl.when(~diagonal)
        def _():
            for part in range(2):
                j = 2 * m + part
                here = xg.at[2 + a, j]
                pltpu.make_async_copy(here, here, rk.at[j]).wait()
                for flag, copy in column_copies(m, part, here, first, d):
                    @pl.when(flag)
                    def _():
                        copy.start()
                remote(here, here, sc.at[j], rc.at[j], near["co"]).start()

    rest = row_steps(1)
    for run in rest[:3]:
        run()
    column_step(0)
    for run in rest[3:6]:
        run()
    column_step(1)
    rest[6]()
    column_step(2)
    column_step(3)

    for xs in range(2):
        for ys in range(4):
            arrived(1, slot(xs, ys, 1 - a))
    keep_l.wait()
    swap.wait()

    @pl.when(diagonal)
    def _():
        for m in range(4):
            for part in range(2):
                for flag, copy in column_copies(m, part, xg.at[a, 2 * m + part], true, 0 * d):
                    @pl.when(flag)
                    def _():
                        copy.wait_send()

    @pl.when(~diagonal)
    def _():
        for m in range(4):
            for part in range(2):
                j = 2 * m + part
                here = xg.at[2 + a, j]
                for flag, copy in column_copies(m, part, here, first, d):
                    @pl.when(flag)
                    def _():
                        copy.wait_send()
                other = xg.at[3 - a, j]
                remote(here, here, sc.at[j], rc.at[j], near["co"]).wait_send()
                pltpu.make_async_copy(other, other, rc.at[j]).wait()

    for copy in started:
        copy.wait_send()


def gather(centers, inverse, downdates):
    dma = pltpu.SemaphoreType.DMA
    anywhere = pl.BlockSpec(memory_space=pl.ANY)
    vmem = pl.BlockSpec(memory_space=pltpu.VMEM)
    width = centers.shape[1]
    rows = inverse.shape[0]
    return pl.pallas_call(
        gather_kernel,
        out_shape=(
            jax.ShapeDtypeStruct((4, 8, FEAT, width), F32),
            jax.ShapeDtypeStruct((16, rows, PANEL), F32),
            jax.ShapeDtypeStruct((PANEL, PANEL), F32),
        ),
        in_specs=[vmem, vmem, anywhere],
        out_specs=(anywhere, anywhere, anywhere),
        scratch_shapes=[
            dma((2,)),
            dma((16,)),
            dma((16,)),
            dma((8,)),
            dma((8,)),
            dma((4, 16)),
            dma((4, 16)),
            dma((3, 8)),
            dma((8,)),
            dma((2,)),
        ],
        compiler_params=pltpu.CompilerParams(collective_id=0, has_side_effects=True),
        name="gather",
    )(centers, inverse, downdates)


def split(value):
    high = value.astype(BF16)
    low = (value - high.astype(F32)).astype(BF16)
    return high, low


def product(left, right, dims):
    dot = functools.partial(lax.dot_general, dimension_numbers=((dims), ((), ())), preferred_element_type=F32)
    (lh, ll), (rh, rl) = left, right
    return dot(lh, rh) + (dot(lh, rl) + dot(ll, rh))


def set_right(x_ref, high, low, norm):
    width = x_ref.shape[-1]
    for j in range(8):
        block = x_ref[0, j]
        norm[:, j * width : (j + 1) * width] = jnp.sum(block * block, axis=0, keepdims=True)
        block = jnp.concatenate([block, jnp.zeros((KPAD - FEAT, width), F32)], axis=0)
        h, l = split(block)
        high[:, j * width : (j + 1) * width] = h
        low[:, j * width : (j + 1) * width] = l


def gauss_tile(left_ref, high, low, norm):
    left = [left_ref[0, j] for j in range(left_ref.shape[1])]
    width = left[0].shape[1]
    zero = jnp.zeros((KPAD - FEAT, width), F32)
    left = jnp.concatenate([jnp.concatenate([block, zero], axis=0).T for block in left], axis=0)
    left_norm = jnp.sum(left * left, axis=1, keepdims=True)
    cross = product(split(left), (high[...], low[...]), ((1,), (0,)))
    return jnp.exp(-(0.5 / FEAT) * (left_norm + norm[...] - 2.0 * cross))


def factor_kernel(s_ref, xl_ref, xr_ref, li_ref, d_ref, dx_ref, out_ref, high, low, norm, lih, lil):
    @pl.when(pl.program_id(0) == 0)
    def _():
        set_right(xr_ref, high, low, norm)
        h, l = split(li_ref[...])
        lih[...] = h
        lil[...] = l

    raw = gauss_tile(xl_ref, high, low, norm) + jnp.where(s_ref[2] == 1, d_ref[...], dx_ref[...])
    result = product(split(raw), (lih[...], lil[...]), ((1,), (1,)))
    out_ref[...] = jnp.where(s_ref[3] == 1, result, 0.0)


TILE = 256


def panel_factor(scalars, xg, li, downdates, dx):
    per = TILE // xg.shape[-1]
    spec = pltpu.PrefetchScalarGridSpec(
        num_scalar_prefetch=1,
        grid=(PANEL // TILE,),
        in_specs=[
            pl.BlockSpec((1, per, FEAT, xg.shape[-1]), lambda i, s: (s[0], i, 0, 0)),
            pl.BlockSpec((1, 8, FEAT, xg.shape[-1]), lambda i, s: (s[1], 0, 0, 0)),
            pl.BlockSpec((PANEL, PANEL), lambda i, s: (0, 0)),
            pl.BlockSpec((TILE, PANEL), lambda i, s: (s[0] * (PANEL // TILE) + i, 0)),
            pl.BlockSpec((TILE, PANEL), lambda i, s: (i, 0)),
        ],
        out_specs=pl.BlockSpec((TILE, PANEL), lambda i, s: (i, 0)),
        scratch_shapes=[
            pltpu.VMEM((KPAD, PANEL), BF16),
            pltpu.VMEM((KPAD, PANEL), BF16),
            pltpu.VMEM((1, PANEL), F32),
            pltpu.VMEM((PANEL, PANEL), BF16),
            pltpu.VMEM((PANEL, PANEL), BF16),
        ],
    )
    return pl.pallas_call(
        factor_kernel, grid_spec=spec, out_shape=jax.ShapeDtypeStruct((PANEL, PANEL), F32), name="factor"
    )(scalars, xg, xg, li, downdates, dx)


def remaining_kernel(s_ref, xl_ref, xr_ref, fl_ref, fr_ref, piece_ref, d_ref, out_ref, piece_out, high, low, norm, frh, frl):
    @pl.when(pl.program_id(0) == 0)
    def _():
        set_right(xr_ref, high, low, norm)
        h, l = split(fr_ref[0])
        frh[...] = h
        frl[...] = l
        piece_out[...] = piece_ref[0]

    update = product(split(fl_ref[0]), (frh[...], frl[...]), ((1,), (1,)))
    out_ref[...] = gauss_tile(xl_ref, high, low, norm) + d_ref[...] - update


def remaining_matrix(scalars, xg, factors, downdates):
    rows = downdates.shape[0]
    width = xg.shape[-1]
    per = TILE // width
    steps = PANEL // TILE
    spec = pltpu.PrefetchScalarGridSpec(
        num_scalar_prefetch=1,
        grid=(rows // TILE,),
        in_specs=[
            pl.BlockSpec((1, per, FEAT, width), lambda i, s: (i // steps, i % steps, 0, 0)),
            pl.BlockSpec((1, 8, FEAT, width), lambda i, s: (s[4], 0, 0, 0)),
            pl.BlockSpec((1, TILE, PANEL), lambda i, s: (i // steps, i % steps, 0)),
            pl.BlockSpec((1, PANEL, PANEL), lambda i, s: (s[5], 0, 0)),
            pl.BlockSpec((1, width, PANEL), lambda i, s: (s[6], s[7], 0)),
            pl.BlockSpec((TILE, PANEL), lambda i, s: (i, 0)),
        ],
        out_specs=(
            pl.BlockSpec((TILE, PANEL), lambda i, s: (i, 0)),
            pl.BlockSpec((width, PANEL), lambda i, s: (0, 0)),
        ),
        scratch_shapes=[
            pltpu.VMEM((KPAD, PANEL), BF16),
            pltpu.VMEM((KPAD, PANEL), BF16),
            pltpu.VMEM((1, PANEL), F32),
            pltpu.VMEM((PANEL, PANEL), BF16),
            pltpu.VMEM((PANEL, PANEL), BF16),
        ],
    )
    return pl.pallas_call(
        remaining_kernel,
        grid_spec=spec,
        out_shape=(
            jax.ShapeDtypeStruct((rows, PANEL), F32),
            jax.ShapeDtypeStruct((width, PANEL), F32),
        ),
        name="remaining",
    )(scalars, xg, xg, factors, factors, factors, downdates)


def spread_kernel(root, f_ref, g, rrow, rcol, rcore, srow, scol, score):
    p = place()
    near = neighbours(p)
    a = p["a"]
    size = PANEL // (2 * CHUNKS)
    y0, x0 = root % 4, root // 4
    d_row = (p["y"] - y0 + 4) % 4
    first_row = p["xl"] == x0
    is_root = first_row & (d_row == 0)
    d_col, first_col, diagonal = column_state(p)
    true = d_col >= 0
    entry_barrier(near)

    def rows(i):
        return pl.ds(pl.multiple_of(i * size, size), size)

    @pl.when(is_root)
    def _():
        def keep(i, carry):
            pltpu.make_async_copy(f_ref.at[rows(i)], g.at[a, rows(i)], rrow.at[i]).start()
            return carry

        lax.fori_loop(0, 2 * CHUNKS, keep, 0)

    def row_copies(m, part):
        i = m + part * CHUNKS
        here = g.at[a, rows(i)]
        flags = branch_flags(first_row, d_row, m, part)
        out = [
            (flag, remote(here, here, srow.at[n, i], rrow.at[i], near[way]))
            for n, (flag, way) in enumerate(zip(flags, ("yp", "ym", "xp")))
        ]
        out.append((true, remote(here, here, score.at[i], rcore.at[i], near["co"])))
        return out

    def column_copies(m, part, from_row):
        i = m + part * CHUNKS
        src = g.at[a, rows(i)] if from_row else g.at[2, rows(i)]
        dst = g.at[2, rows(i)]
        flags = branch_flags(true, 0 * d_col, m, part) if from_row else branch_flags(first_col, d_col, m, part)
        return [
            (flag, remote(src, dst, scol.at[n, i], rcol.at[i], near[way]))
            for n, (flag, way) in enumerate(zip(flags, ("zp", "zm", "xx")))
        ]

    def each(copies, act):
        for flag, copy in copies:
            @pl.when(flag)
            def _():
                act(copy)

    def row_step(m):
        for part in range(2):
            i = m + part * CHUNKS
            here = g.at[a, rows(i)]
            pltpu.make_async_copy(here, here, rrow.at[i]).wait()
            each(row_copies(m, part), lambda copy: copy.start())

            @pl.when(diagonal)
            def _():
                each(column_copies(m, part, True), lambda copy: copy.start())

    def column_step(m):
        @pl.when(~diagonal)
        def _():
            for part in range(2):
                i = m + part * CHUNKS
                here = g.at[2, rows(i)]
                pltpu.make_async_copy(here, here, rcol.at[i]).wait()
                each(column_copies(m, part, False), lambda copy: copy.start())

    def loop(low, high, body):
        def run(m, carry):
            body(m)
            return carry

        lax.fori_loop(low, high, run, 0)

    loop(0, LAG, row_step)

    def both(m):
        row_step(m)
        column_step(m - LAG)

    loop(LAG, CHUNKS, both)
    loop(CHUNKS - LAG, CHUNKS, column_step)

    def finish(m):
        for part in range(2):
            i = m + part * CHUNKS
            there = g.at[1 - a, rows(i)]
            pltpu.make_async_copy(there, there, rcore.at[i]).wait()
            each(row_copies(m, part), lambda copy: copy.wait_send())

            @pl.when(diagonal)
            def _():
                each(column_copies(m, part, True), lambda copy: copy.wait_send())

            @pl.when(~diagonal)
            def _():
                each(column_copies(m, part, False), lambda copy: copy.wait_send())

    loop(0, CHUNKS, finish)


def spread(root, half):
    dma = pltpu.SemaphoreType.DMA
    n = 2 * CHUNKS
    return pl.pallas_call(
        functools.partial(spread_kernel, root),
        out_shape=jax.ShapeDtypeStruct((3, PANEL, PANEL), F32),
        in_specs=[pl.BlockSpec(memory_space=pltpu.VMEM)],
        out_specs=pl.BlockSpec(memory_space=pl.ANY),
        scratch_shapes=[dma((n,)), dma((n,)), dma((n,)), dma((3, n)), dma((3, n)), dma((n,))],
        compiler_params=pltpu.CompilerParams(collective_id=1 + root, has_side_effects=True),
        name="spread" + str(root),
    )(half)


def shards(downdates, centers, diag_inverse, block_map, panel_index):
    row = lax.axis_index("row")
    col = lax.axis_index("col")
    core = col % 2
    diagonal = row == col // 2
    block_ids = jnp.arange(BLOCKS, dtype=jnp.int32)
    panel_block = jnp.sum(block_ids * (block_map == panel_index[0]).astype(jnp.int32))
    alive = jnp.sum(jnp.where(block_ids == 2 * row + core, block_map, 0)) > panel_index[0]
    base = jnp.where(diagonal, 0, 2)
    scalars = jnp.stack(
        [
            core,
            base + panel_block % 2,
            (panel_block % 2 == core).astype(jnp.int32),
            alive.astype(jnp.int32),
            base + core,
            jnp.where(diagonal, core, 2),
            col // 8,
            col % 8,
        ]
    ).astype(jnp.int32)
    xg, li, dx = gather(centers, diag_inverse, downdates)
    half = panel_factor(scalars, xg, li.reshape(PANEL, PANEL), downdates, dx)
    factors = lax.switch(panel_block // 2, [functools.partial(spread, root) for root in range(BLOCKS // 2)], half)
    remaining, piece = remaining_matrix(scalars, xg, factors, downdates)
    return piece, remaining


def solution(mesh):
    return jax.shard_map(
        shards,
        mesh=mesh,
        in_specs=(P("row", "col"), P(None, ("row", "col")), P("col", None), P(), P()),
        out_specs=(P(("row", "col"), None), P("row", "col")),
        check_vma=False,
    )
```

```python
import functools

import jax
import jax.numpy as jnp
from jax import lax
from jax.experimental import pallas as pl
from jax.experimental.pallas import tpu as pltpu
from jax.sharding import PartitionSpec as P

PANEL = 1024
FEAT = 440
KPAD = 512
BLOCKS = 16
MESH = pl.DeviceIdType.MESH
F32 = jnp.float32
BF16 = jnp.bfloat16
CHUNKS = 32
SKEW = 2


def place():
    row = lax.axis_index("row")
    col = lax.axis_index("col")
    return dict(z=row // 2, xh=row % 2, xl=col // 8, y=(col // 2) % 4, a=col % 2)


def device(p, **changes):
    q = dict(p)
    q.update(changes)
    return (q["z"] * 2 + q["xh"], q["xl"] * 8 + q["y"] * 2 + q["a"])


def neighbours(p):
    return dict(
        yp=device(p, y=(p["y"] + 1) % 4),
        ym=device(p, y=(p["y"] + 3) % 4),
        xp=device(p, xl=1 - p["xl"]),
        zp=device(p, z=(p["z"] + 1) % 4),
        zm=device(p, z=(p["z"] + 3) % 4),
        xx=device(p, xh=1 - p["xh"]),
        co=device(p, a=1 - p["a"]),
    )


def entry_barrier(near):
    barrier = pltpu.get_barrier_semaphore()
    for where in near.values():
        pl.semaphore_signal(barrier, inc=1, device_id=where, device_id_type=MESH)
    pl.semaphore_wait(barrier, len(near))


def remote(src, dst, send, recv, where):
    return pltpu.make_async_remote_copy(
        src_ref=src, dst_ref=dst, send_sem=send, recv_sem=recv, device_id=where, device_id_type=MESH
    )


def branch_flags(first_ring, d, m, part):
    rel = (d - m + 16) % 4
    if part == 0:
        up = (first_ring & (d != 3)) | (~first_ring & (rel <= 1))
        down = ~first_ring & (rel == 0)
    else:
        up = ~first_ring & (rel == 0)
        down = (first_ring & (d != 1)) | (~first_ring & ((rel == 0) | (rel == 3)))
    across = first_ring & (rel == 0)
    return up, down, across


def column_state(p):
    k = p["xl"] * 4 + p["y"]
    d = (p["z"] - k // 2 + 4) % 4
    first = p["xh"] == k % 2
    diagonal = (p["z"] * 2 + p["xh"]) == k
    return d, first, diagonal


def gather_kernel(x_ref, l_ref, d_ref, xg, li, dx, own, rx, rl, rk, rc, sx, sl, sk, sc, sd):
    p = place()
    near = neighbours(p)
    a, y, xl = p["a"], p["y"], p["xl"]
    d, first, diagonal = column_state(p)
    entry_barrier(near)

    def slot(xl_, y_, a_):
        return xl_ * 8 + y_ * 2 + a_

    def at(table, s):
        return xg.at[s // 8, s % 8] if table == 0 else li.at[s]

    started = []

    def send(table, s, way, src=None):
        src = at(table, s) if src is None else src
        sems, recv = (sx, rx) if table == 0 else (sl, rl)
        way_index = ("yp", "ym", "xp", "co").index(way)
        copy = remote(src, at(table, s), sems.at[way_index, s], recv.at[s], near[way])
        copy.start()
        started.append(copy)

    def arrived(table, s):
        recv = rx if table == 0 else rl
        copy = pltpu.make_async_copy(at(table, s), at(table, s), recv.at[s])
        copy.wait()

    mine = slot(xl, y, a)
    before, after, far = (y + 3) % 4, (y + 1) % 4, (y + 2) % 4

    def first_sends(table):
        src = x_ref if table == 0 else l_ref
        for way in ("yp", "ym", "xp", "co"):
            send(table, mine, way, src)
        keep = pltpu.make_async_copy(src, at(table, mine), own.at[table])
        keep.start()
        return keep

    keep_x = first_sends(0)
    keep_l = first_sends(1)
    half = PANEL
    swap = remote(d_ref.at[pl.ds((1 - a) * half, half)], dx, sd.at[0], sd.at[1], near["co"])
    swap.start()

    def row_steps(table):
        steps = []

        def step(s, *ways):
            def run():
                arrived(table, s)
                for way in ways:
                    send(table, s, way)

            steps.append(run)

        step(slot(1 - xl, y, a), "yp", "ym", "co")
        if table == 0:
            step(slot(xl, before, a), "yp", "co")
            step(slot(xl, after, a), "co")
        else:
            step(slot(xl, after, a), "ym", "co")
            step(slot(xl, before, a), "co")
        step(slot(1 - xl, before, a), "co")
        step(slot(1 - xl, after, a), "co")
        step(slot(xl, far, a), "xp", "co")
        step(slot(1 - xl, far, a), "co")
        return steps

    for run in row_steps(0):
        run()
    for xs in range(2):
        for ys in range(4):
            arrived(0, slot(xs, ys, 1 - a))
    keep_x.wait()

    def column_copies(m, part, src, is_first, dist):
        up, down, across = branch_flags(is_first, dist, m, part)
        j = 2 * m + part
        dst = xg.at[2 + a, j]
        out = []
        for index, (flag, way) in enumerate(((up, "zp"), (down, "zm"), (across, "xx"))):
            out.append((flag, remote(src, dst, sk.at[index, j], rk.at[j], near[way])))
        return out

    true = d >= 0

    @pl.when(diagonal)
    def _():
        for m in range(4):
            for part in range(2):
                for flag, copy in column_copies(m, part, xg.at[a, 2 * m + part], true, 0 * d):
                    @pl.when(flag)
                    def _():
                        copy.start()

    def column_step(m):
        @pl.when(~diagonal)
        def _():
            for part in range(2):
                j = 2 * m + part
                here = xg.at[2 + a, j]
                pltpu.make_async_copy(here, here, rk.at[j]).wait()
                for flag, copy in column_copies(m, part, here, first, d):
                    @pl.when(flag)
                    def _():
                        copy.start()
                remote(here, here, sc.at[j], rc.at[j], near["co"]).start()

    rest = row_steps(1)
    for run in rest[:3]:
        run()
    column_step(0)
    for run in rest[3:6]:
        run()
    column_step(1)
    rest[6]()
    column_step(2)
    column_step(3)

    for xs in range(2):
        for ys in range(4):
            arrived(1, slot(xs, ys, 1 - a))
    keep_l.wait()
    swap.wait()

    @pl.when(diagonal)
    def _():
        for m in range(4):
            for part in range(2):
                for flag, copy in column_copies(m, part, xg.at[a, 2 * m + part], true, 0 * d):
                    @pl.when(flag)
                    def _():
                        copy.wait_send()

    @pl.when(~diagonal)
    def _():
        for m in range(4):
            for part in range(2):
                j = 2 * m + part
                here = xg.at[2 + a, j]
                for flag, copy in column_copies(m, part, here, first, d):
                    @pl.when(flag)
                    def _():
                        copy.wait_send()
                other = xg.at[3 - a, j]
                remote(here, here, sc.at[j], rc.at[j], near["co"]).wait_send()
                pltpu.make_async_copy(other, other, rc.at[j]).wait()

    for copy in started:
        copy.wait_send()


def gather(centers, inverse, downdates):
    dma = pltpu.SemaphoreType.DMA
    anywhere = pl.BlockSpec(memory_space=pl.ANY)
    vmem = pl.BlockSpec(memory_space=pltpu.VMEM)
    width = centers.shape[1]
    rows = inverse.shape[0]
    return pl.pallas_call(
        gather_kernel,
        out_shape=(
            jax.ShapeDtypeStruct((4, 8, FEAT, width), F32),
            jax.ShapeDtypeStruct((16, rows, PANEL), F32),
            jax.ShapeDtypeStruct((PANEL, PANEL), F32),
        ),
        in_specs=[vmem, vmem, anywhere],
        out_specs=(anywhere, anywhere, anywhere),
        scratch_shapes=[
            dma((2,)),
            dma((16,)),
            dma((16,)),
            dma((8,)),
            dma((8,)),
            dma((4, 16)),
            dma((4, 16)),
            dma((3, 8)),
            dma((8,)),
            dma((2,)),
        ],
        compiler_params=pltpu.CompilerParams(collective_id=0, has_side_effects=True),
        name="gather",
    )(centers, inverse, downdates)


def split(value):
    high = value.astype(BF16)
    low = (value - high.astype(F32)).astype(BF16)
    return high, low


def product(left, right, dims):
    dot = functools.partial(lax.dot_general, dimension_numbers=((dims), ((), ())), preferred_element_type=F32)
    (lh, ll), (rh, rl) = left, right
    return dot(lh, rh) + (dot(lh, rl) + dot(ll, rh))


def set_right(x_ref, high, low, norm):
    width = x_ref.shape[-1]
    for j in range(8):
        block = x_ref[0, j]
        norm[:, j * width : (j + 1) * width] = jnp.sum(block * block, axis=0, keepdims=True)
        block = jnp.concatenate([block, jnp.zeros((KPAD - FEAT, width), F32)], axis=0)
        h, l = split(block)
        high[:, j * width : (j + 1) * width] = h
        low[:, j * width : (j + 1) * width] = l


def gauss_tile(left_ref, high, low, norm):
    left = [left_ref[0, j] for j in range(left_ref.shape[1])]
    width = left[0].shape[1]
    zero = jnp.zeros((KPAD - FEAT, width), F32)
    left = jnp.concatenate([jnp.concatenate([block, zero], axis=0).T for block in left], axis=0)
    left_norm = jnp.sum(left * left, axis=1, keepdims=True)
    cross = product(split(left), (high[...], low[...]), ((1,), (0,)))
    return jnp.exp(-(0.5 / FEAT) * (left_norm + norm[...] - 2.0 * cross))


def factor_kernel(s_ref, xl_ref, xr_ref, li_ref, d_ref, dx_ref, out_ref, high, low, norm, lih, lil):
    @pl.when(pl.program_id(0) == 0)
    def _():
        set_right(xr_ref, high, low, norm)
        h, l = split(li_ref[...])
        lih[...] = h
        lil[...] = l

    raw = gauss_tile(xl_ref, high, low, norm) + jnp.where(s_ref[2] == 1, d_ref[...], dx_ref[...])
    result = product(split(raw), (lih[...], lil[...]), ((1,), (1,)))
    out_ref[...] = jnp.where(s_ref[3] == 1, result, 0.0)


TILE = 256


def panel_factor(scalars, xg, li, downdates, dx):
    per = TILE // xg.shape[-1]
    spec = pltpu.PrefetchScalarGridSpec(
        num_scalar_prefetch=1,
        grid=(PANEL // TILE,),
        in_specs=[
            pl.BlockSpec((1, per, FEAT, xg.shape[-1]), lambda i, s: (s[0], i, 0, 0)),
            pl.BlockSpec((1, 8, FEAT, xg.shape[-1]), lambda i, s: (s[1], 0, 0, 0)),
            pl.BlockSpec((PANEL, PANEL), lambda i, s: (0, 0)),
            pl.BlockSpec((TILE, PANEL), lambda i, s: (s[0] * (PANEL // TILE) + i, 0)),
            pl.BlockSpec((TILE, PANEL), lambda i, s: (i, 0)),
        ],
        out_specs=pl.BlockSpec((TILE, PANEL), lambda i, s: (i, 0)),
        scratch_shapes=[
            pltpu.VMEM((KPAD, PANEL), BF16),
            pltpu.VMEM((KPAD, PANEL), BF16),
            pltpu.VMEM((1, PANEL), F32),
            pltpu.VMEM((PANEL, PANEL), BF16),
            pltpu.VMEM((PANEL, PANEL), BF16),
        ],
    )
    return pl.pallas_call(
        factor_kernel, grid_spec=spec, out_shape=jax.ShapeDtypeStruct((PANEL, PANEL), F32), name="factor"
    )(scalars, xg, xg, li, downdates, dx)


def remaining_kernel(s_ref, xl_ref, xr_ref, fl_ref, fr_ref, piece_ref, d_ref, out_ref, piece_out, high, low, norm, frh, frl):
    @pl.when(pl.program_id(0) == 0)
    def _():
        set_right(xr_ref, high, low, norm)
        h, l = split(fr_ref[0])
        frh[...] = h
        frl[...] = l
        piece_out[...] = piece_ref[0]

    update = product(split(fl_ref[0]), (frh[...], frl[...]), ((1,), (1,)))
    out_ref[...] = gauss_tile(xl_ref, high, low, norm) + d_ref[...] - update


def remaining_matrix(scalars, xg, factors, downdates):
    rows = downdates.shape[0]
    width = xg.shape[-1]
    per = TILE // width
    steps = PANEL // TILE
    spec = pltpu.PrefetchScalarGridSpec(
        num_scalar_prefetch=1,
        grid=(rows // TILE,),
        in_specs=[
            pl.BlockSpec((1, per, FEAT, width), lambda i, s: (i // steps, i % steps, 0, 0)),
            pl.BlockSpec((1, 8, FEAT, width), lambda i, s: (s[4], 0, 0, 0)),
            pl.BlockSpec((1, TILE, PANEL), lambda i, s: (i // steps, i % steps, 0)),
            pl.BlockSpec((1, PANEL, PANEL), lambda i, s: (s[5], 0, 0)),
            pl.BlockSpec((1, width, PANEL), lambda i, s: (s[6], s[7], 0)),
            pl.BlockSpec((TILE, PANEL), lambda i, s: (i, 0)),
        ],
        out_specs=(
            pl.BlockSpec((TILE, PANEL), lambda i, s: (i, 0)),
            pl.BlockSpec((width, PANEL), lambda i, s: (0, 0)),
        ),
        scratch_shapes=[
            pltpu.VMEM((KPAD, PANEL), BF16),
            pltpu.VMEM((KPAD, PANEL), BF16),
            pltpu.VMEM((1, PANEL), F32),
            pltpu.VMEM((PANEL, PANEL), BF16),
            pltpu.VMEM((PANEL, PANEL), BF16),
        ],
    )
    return pl.pallas_call(
        remaining_kernel,
        grid_spec=spec,
        out_shape=(
            jax.ShapeDtypeStruct((rows, PANEL), F32),
            jax.ShapeDtypeStruct((width, PANEL), F32),
        ),
        name="remaining",
    )(scalars, xg, xg, factors, factors, factors, downdates)


def hops(first_ring, d, e, part):
    rel = (d - e + 4) % 4
    near_e = e if part == 0 else (4 - e) % 4
    in_first = d if part == 0 else (4 - d) % 4
    return jnp.where(first_ring, in_first, near_e + 1 + jnp.minimum(rel, 4 - rel))


def spread_kernel(root, f_ref, g, rrow, rcol, rcore, srow, scol, score):
    p = place()
    near = neighbours(p)
    a = p["a"]
    size = PANEL // (2 * CHUNKS)
    y0, x0 = root % 4, root // 4
    d_row = (p["y"] - y0 + 4) % 4
    first_row = p["xl"] == x0
    is_root = first_row & (d_row == 0)
    d_col, first_col, diagonal = column_state(p)
    true = d_col >= 0
    entry_barrier(near)

    def rows(i):
        return pl.ds(pl.multiple_of(i * size, size), size)

    @pl.when(is_root)
    def _():
        def keep(i, carry):
            pltpu.make_async_copy(f_ref.at[rows(i)], g.at[a, rows(i)], rrow.at[i]).start()
            return carry

        lax.fori_loop(0, 2 * CHUNKS, keep, 0)

    def row_copies(m, e, part):
        i = m + part * CHUNKS
        here = g.at[a, rows(i)]
        flags = branch_flags(first_row, d_row, e, part)
        out = [
            (flag, remote(here, here, srow.at[n, i], rrow.at[i], near[way]))
            for n, (flag, way) in enumerate(zip(flags, ("yp", "ym", "xp")))
        ]
        out.append((true, remote(here, here, score.at[i], rcore.at[i], near["co"])))
        return out

    def column_copies(m, e, part, from_row):
        i = m + part * CHUNKS
        src = g.at[a, rows(i)] if from_row else g.at[2, rows(i)]
        dst = g.at[2, rows(i)]
        flags = branch_flags(true, 0 * d_col, e, part) if from_row else branch_flags(first_col, d_col, e, part)
        return [
            (flag, remote(src, dst, scol.at[n, i], rcol.at[i], near[way]))
            for n, (flag, way) in enumerate(zip(flags, ("zp", "zm", "xx")))
        ]

    def each(copies, act):
        for flag, copy in copies:
            @pl.when(flag)
            def _():
                act(copy)

    row_lag = {}
    col_lag = {}
    for e in range(4):
        for part in range(2):
            row_lag[e, part] = SKEW * hops(first_row, d_row, e, part)
            col_lag[e, part] = row_lag[e, part] + SKEW * hops(first_col, d_col, e, part)

    def turn(t, carry):
        for e in range(4):
            for part in range(2):
                m = t - row_lag[e, part]

                @pl.when((m >= 0) & (m < CHUNKS) & ((m + 64) % 4 == e))
                def _():
                    i = m + part * CHUNKS
                    here = g.at[a, rows(i)]
                    pltpu.make_async_copy(here, here, rrow.at[i]).wait()
                    each(row_copies(m, e, part), lambda copy: copy.start())

                    @pl.when(diagonal)
                    def _():
                        each(column_copies(m, e, part, True), lambda copy: copy.start())

                n = t - col_lag[e, part]

                @pl.when((n >= 0) & (n < CHUNKS) & ((n + 64) % 4 == e) & ~diagonal)
                def _():
                    i = n + part * CHUNKS
                    here = g.at[2, rows(i)]
                    pltpu.make_async_copy(here, here, rcol.at[i]).wait()
                    each(column_copies(n, e, part, False), lambda copy: copy.start())

        return carry

    lax.fori_loop(0, CHUNKS + 12 * SKEW, turn, 0)

    def finish(group, carry):
        for e in range(4):
            m = group * 4 + e
            for part in range(2):
                i = m + part * CHUNKS
                there = g.at[1 - a, rows(i)]
                pltpu.make_async_copy(there, there, rcore.at[i]).wait()
                each(row_copies(m, e, part), lambda copy: copy.wait_send())

                @pl.when(diagonal)
                def _():
                    each(column_copies(m, e, part, True), lambda copy: copy.wait_send())

                @pl.when(~diagonal)
                def _():
                    each(column_copies(m, e, part, False), lambda copy: copy.wait_send())

        return carry

    lax.fori_loop(0, CHUNKS // 4, finish, 0)


def spread(root, half):
    dma = pltpu.SemaphoreType.DMA
    n = 2 * CHUNKS
    return pl.pallas_call(
        functools.partial(spread_kernel, root),
        out_shape=jax.ShapeDtypeStruct((3, PANEL, PANEL), F32),
        in_specs=[pl.BlockSpec(memory_space=pltpu.VMEM)],
        out_specs=pl.BlockSpec(memory_space=pl.ANY),
        scratch_shapes=[dma((n,)), dma((n,)), dma((n,)), dma((3, n)), dma((3, n)), dma((n,))],
        compiler_params=pltpu.CompilerParams(collective_id=1 + root, has_side_effects=True),
        name="spread" + str(root),
    )(half)


def shards(downdates, centers, diag_inverse, block_map, panel_index):
    row = lax.axis_index("row")
    col = lax.axis_index("col")
    core = col % 2
    diagonal = row == col // 2
    block_ids = jnp.arange(BLOCKS, dtype=jnp.int32)
    panel_block = jnp.sum(block_ids * (block_map == panel_index[0]).astype(jnp.int32))
    alive = jnp.sum(jnp.where(block_ids == 2 * row + core, block_map, 0)) > panel_index[0]
    base = jnp.where(diagonal, 0, 2)
    scalars = jnp.stack(
        [
            core,
            base + panel_block % 2,
            (panel_block % 2 == core).astype(jnp.int32),
            alive.astype(jnp.int32),
            base + core,
            jnp.where(diagonal, core, 2),
            col // 8,
            col % 8,
        ]
    ).astype(jnp.int32)
    xg, li, dx = gather(centers, diag_inverse, downdates)
    half = panel_factor(scalars, xg, li.reshape(PANEL, PANEL), downdates, dx)
    factors = lax.switch(panel_block // 2, [functools.partial(spread, root) for root in range(BLOCKS // 2)], half)
    remaining, piece = remaining_matrix(scalars, xg, factors, downdates)
    return piece, remaining


def solution(mesh):
    return jax.shard_map(
        shards,
        mesh=mesh,
        in_specs=(P("row", "col"), P(None, ("row", "col")), P("col", None), P(), P()),
        out_specs=(P(("row", "col"), None), P("row", "col")),
        check_vma=False,
    )
```

```python
import functools

import jax
import jax.numpy as jnp
from jax import lax
from jax.experimental import pallas as pl
from jax.experimental.pallas import tpu as pltpu
from jax.sharding import PartitionSpec as P

PANEL = 1024
FEAT = 440
KPAD = 512
BLOCKS = 16
MESH = pl.DeviceIdType.MESH
F32 = jnp.float32
BF16 = jnp.bfloat16
CHUNKS = 64
SKEW = 4
PIECES = 5
CENTER_SKEW = 3


def place():
    row = lax.axis_index("row")
    col = lax.axis_index("col")
    return dict(z=row // 2, xh=row % 2, xl=col // 8, y=(col // 2) % 4, a=col % 2)


def device(p, **changes):
    q = dict(p)
    q.update(changes)
    return (q["z"] * 2 + q["xh"], q["xl"] * 8 + q["y"] * 2 + q["a"])


def neighbours(p):
    return dict(
        yp=device(p, y=(p["y"] + 1) % 4),
        ym=device(p, y=(p["y"] + 3) % 4),
        xp=device(p, xl=1 - p["xl"]),
        zp=device(p, z=(p["z"] + 1) % 4),
        zm=device(p, z=(p["z"] + 3) % 4),
        xx=device(p, xh=1 - p["xh"]),
        co=device(p, a=1 - p["a"]),
    )


def entry_barrier(near):
    barrier = pltpu.get_barrier_semaphore()
    for where in near.values():
        pl.semaphore_signal(barrier, inc=1, device_id=where, device_id_type=MESH)
    pl.semaphore_wait(barrier, len(near))


def remote(src, dst, send, recv, where):
    return pltpu.make_async_remote_copy(
        src_ref=src, dst_ref=dst, send_sem=send, recv_sem=recv, device_id=where, device_id_type=MESH
    )


def branch_flags(first_ring, d, m, part):
    rel = (d - m + 16) % 4
    if part == 0:
        up = (first_ring & (d != 3)) | (~first_ring & (rel <= 1))
        down = ~first_ring & (rel == 0)
    else:
        up = ~first_ring & (rel == 0)
        down = (first_ring & (d != 1)) | (~first_ring & ((rel == 0) | (rel == 3)))
    across = first_ring & (rel == 0)
    return up, down, across


def hops(first_ring, d, e, part):
    rel = (d - e + 4) % 4
    near_e = e if part == 0 else (4 - e) % 4
    in_first = d if part == 0 else (4 - d) % 4
    return jnp.where(first_ring, in_first, near_e + 1 + jnp.minimum(rel, 4 - rel))


def column_state(p):
    k = p["xl"] * 4 + p["y"]
    d = (p["z"] - k // 2 + 4) % 4
    first = p["xh"] == k % 2
    diagonal = (p["z"] * 2 + p["xh"]) == k
    return d, first, diagonal


def gather_kernel(x_ref, l_ref, d_ref, xg, li, dx, own, rx, rl, rk, rc, sx, sl, sk, sc, sd):
    p = place()
    near = neighbours(p)
    a, y, xl = p["a"], p["y"], p["xl"]
    d, first, diagonal = column_state(p)
    entry_barrier(near)

    def slot(xl_, y_, a_):
        return xl_ * 8 + y_ * 2 + a_

    def at(table, s):
        return xg.at[s // 8, s % 8] if table == 0 else li.at[s]

    started = []

    def row_copy(table, s, way, src):
        src = at(table, s) if src is None else src
        sems, recv = (sx, rx) if table == 0 else (sl, rl)
        way_index = ("yp", "ym", "xp", "co").index(way)
        return remote(src, at(table, s), sems.at[way_index, s], recv.at[s], near[way])

    def send(table, s, way, src=None):
        row_copy(table, s, way, src).start()
        started.append((table, s, way, src))

    def arrived(table, s):
        recv = rx if table == 0 else rl
        copy = pltpu.make_async_copy(at(table, s), at(table, s), recv.at[s])
        copy.wait()

    mine = slot(xl, y, a)
    before, after, far = (y + 3) % 4, (y + 1) % 4, (y + 2) % 4

    def first_sends(table):
        src = x_ref if table == 0 else l_ref
        for way in ("yp", "ym", "xp", "co"):
            send(table, mine, way, src)
        keep = pltpu.make_async_copy(src, at(table, mine), own.at[table])
        keep.start()
        return keep

    keep_x = first_sends(0)

    def row_steps(table):
        steps = []

        def step(s, *ways):
            def run():
                arrived(table, s)
                for way in ways:
                    send(table, s, way)

            steps.append(run)

        step(slot(1 - xl, y, a), "yp", "ym", "co")
        if table == 0:
            step(slot(xl, before, a), "yp", "co")
            step(slot(xl, after, a), "co")
        else:
            step(slot(xl, after, a), "ym", "co")
            step(slot(xl, before, a), "co")
        step(slot(1 - xl, before, a), "co")
        step(slot(1 - xl, after, a), "co")
        step(slot(xl, far, a), "xp", "co")
        step(slot(1 - xl, far, a), "co")
        return steps

    for run in row_steps(0):
        run()
    for xs in range(2):
        for ys in range(4):
            arrived(0, slot(xs, ys, 1 - a))
    keep_x.wait()

    chunks = 4 * PIECES
    tall = FEAT // PIECES
    true = d >= 0

    def piece(table, n, part):
        return xg.at[table, 2 * (n // PIECES) + part, pl.ds(pl.multiple_of((n % PIECES) * tall, 8), tall)]

    def column_copies(n, e, part, is_root):
        c = part * chunks + n
        src = piece(a, n, part) if is_root else piece(2 + a, n, part)
        flags = branch_flags(true, 0 * d, e, part) if is_root else branch_flags(first, d, e, part)
        return [
            (flag, remote(src, piece(2 + a, n, part), sk.at[index, 2 * e + part], rk.at[c], near[way]))
            for index, (flag, way) in enumerate(zip(flags, ("zp", "zm", "xx")))
        ]

    def core_copy(n, part):
        here = piece(2 + a, n, part)
        return remote(here, here, sc.at[0], rc.at[0], near["co"])

    def each(copies, act):
        for flag, copy in copies:
            @pl.when(flag)
            def _():
                act(copy)

    @pl.when(diagonal)
    def _():
        def issue(group, carry):
            for e in range(4):
                for part in range(2):
                    each(column_copies(4 * group + e, e, part, True), lambda copy: copy.start())
            return carry

        lax.fori_loop(0, PIECES, issue, 0)

    keep_l = first_sends(1)
    half = PANEL
    swap = remote(d_ref.at[pl.ds((1 - a) * half, half)], dx, sd.at[0], sd.at[1], near["co"])
    swap.start()

    lag = {}
    for e in range(4):
        for part in range(2):
            lag[e, part] = CENTER_SKEW * hops(first, d, e, part)

    rest = row_steps(1)
    turns = chunks + 6 * CENTER_SKEW
    cuts = {turns // 5: rest[:3], 2 * turns // 5: rest[3:6], 3 * turns // 5: rest[6:]}

    def turn(t, carry):
        for cut, steps in cuts.items():
            @pl.when(t == cut)
            def _():
                for run in steps:
                    run()

        for e in range(4):
            for part in range(2):
                n = t - lag[e, part]

                @pl.when((n >= 0) & (n < chunks) & ((n + 256) % 4 == e) & ~diagonal)
                def _():
                    here = piece(2 + a, n, part)
                    pltpu.make_async_copy(here, here, rk.at[part * chunks + n]).wait()
                    each(column_copies(n, e, part, False), lambda copy: copy.start())
                    core_copy(n, part).start()

        return carry

    lax.fori_loop(0, turns, turn, 0)

    for xs in range(2):
        for ys in range(4):
            arrived(1, slot(xs, ys, 1 - a))
    keep_l.wait()
    swap.wait()

    def whole(ref, sem):
        pltpu.make_async_copy(ref, ref, sem).wait()

    for e in range(4):
        for part in range(2):
            at_root = branch_flags(true, 0 * d, e, part)
            below = branch_flags(first, d, e, part)
            for index in range(3):
                @pl.when((diagonal & at_root[index]) | (~diagonal & below[index]))
                def _():
                    whole(xg.at[2 + a, 0], sk.at[index, 2 * e + part])

    @pl.when(~diagonal)
    def _():
        whole(xg.at[2 + a], sc.at[0])
        whole(xg.at[3 - a], rc.at[0])

    for copy in started:
        row_copy(*copy).wait_send()


def gather(centers, inverse, downdates):
    dma = pltpu.SemaphoreType.DMA
    anywhere = pl.BlockSpec(memory_space=pl.ANY)
    vmem = pl.BlockSpec(memory_space=pltpu.VMEM)
    width = centers.shape[1]
    rows = inverse.shape[0]
    return pl.pallas_call(
        gather_kernel,
        out_shape=(
            jax.ShapeDtypeStruct((4, 8, FEAT, width), F32),
            jax.ShapeDtypeStruct((16, rows, PANEL), F32),
            jax.ShapeDtypeStruct((PANEL, PANEL), F32),
        ),
        in_specs=[vmem, vmem, anywhere],
        out_specs=(anywhere, anywhere, anywhere),
        scratch_shapes=[
            dma((2,)),
            dma((16,)),
            dma((16,)),
            dma((8 * PIECES,)),
            dma((1,)),
            dma((4, 16)),
            dma((4, 16)),
            dma((3, 8)),
            dma((1,)),
            dma((2,)),
        ],
        compiler_params=pltpu.CompilerParams(collective_id=0, has_side_effects=True),
        name="gather",
    )(centers, inverse, downdates)


def split(value):
    high = value.astype(BF16)
    low = (value - high.astype(F32)).astype(BF16)
    return high, low


def product(left, right, dims):
    dot = functools.partial(lax.dot_general, dimension_numbers=((dims), ((), ())), preferred_element_type=F32)
    (lh, ll), (rh, rl) = left, right
    return dot(lh, rh) + (dot(lh, rl) + dot(ll, rh))


def set_right(x_ref, high, low, norm):
    width = x_ref.shape[-1]
    for j in range(8):
        block = x_ref[0, j]
        norm[:, j * width : (j + 1) * width] = jnp.sum(block * block, axis=0, keepdims=True)
        block = jnp.concatenate([block, jnp.zeros((KPAD - FEAT, width), F32)], axis=0)
        h, l = split(block)
        high[:, j * width : (j + 1) * width] = h
        low[:, j * width : (j + 1) * width] = l


def gauss_tile(left_ref, high, low, norm):
    left = [left_ref[0, j] for j in range(left_ref.shape[1])]
    width = left[0].shape[1]
    zero = jnp.zeros((KPAD - FEAT, width), F32)
    left = jnp.concatenate([jnp.concatenate([block, zero], axis=0).T for block in left], axis=0)
    left_norm = jnp.sum(left * left, axis=1, keepdims=True)
    cross = product(split(left), (high[...], low[...]), ((1,), (0,)))
    return jnp.exp(-(0.5 / FEAT) * (left_norm + norm[...] - 2.0 * cross))


def factor_kernel(s_ref, xl_ref, xr_ref, li_ref, d_ref, dx_ref, out_ref, high, low, norm, lih, lil):
    @pl.when(pl.program_id(0) == 0)
    def _():
        set_right(xr_ref, high, low, norm)
        h, l = split(li_ref[...])
        lih[...] = h
        lil[...] = l

    raw = gauss_tile(xl_ref, high, low, norm) + jnp.where(s_ref[2] == 1, d_ref[...], dx_ref[...])
    result = product(split(raw), (lih[...], lil[...]), ((1,), (1,)))
    out_ref[...] = jnp.where(s_ref[3] == 1, result, 0.0)


TILE = 256


def panel_factor(scalars, xg, li, downdates, dx):
    per = TILE // xg.shape[-1]
    spec = pltpu.PrefetchScalarGridSpec(
        num_scalar_prefetch=1,
        grid=(PANEL // TILE,),
        in_specs=[
            pl.BlockSpec((1, per, FEAT, xg.shape[-1]), lambda i, s: (s[0], i, 0, 0)),
            pl.BlockSpec((1, 8, FEAT, xg.shape[-1]), lambda i, s: (s[1], 0, 0, 0)),
            pl.BlockSpec((PANEL, PANEL), lambda i, s: (0, 0)),
            pl.BlockSpec((TILE, PANEL), lambda i, s: (s[0] * (PANEL // TILE) + i, 0)),
            pl.BlockSpec((TILE, PANEL), lambda i, s: (i, 0)),
        ],
        out_specs=pl.BlockSpec((TILE, PANEL), lambda i, s: (i, 0)),
        scratch_shapes=[
            pltpu.VMEM((KPAD, PANEL), BF16),
            pltpu.VMEM((KPAD, PANEL), BF16),
            pltpu.VMEM((1, PANEL), F32),
            pltpu.VMEM((PANEL, PANEL), BF16),
            pltpu.VMEM((PANEL, PANEL), BF16),
        ],
    )
    return pl.pallas_call(
        factor_kernel, grid_spec=spec, out_shape=jax.ShapeDtypeStruct((PANEL, PANEL), F32), name="factor"
    )(scalars, xg, xg, li, downdates, dx)


def remaining_kernel(s_ref, xl_ref, xr_ref, fl_ref, fr_ref, piece_ref, d_ref, out_ref, piece_out, high, low, norm, frh, frl):
    @pl.when(pl.program_id(0) == 0)
    def _():
        set_right(xr_ref, high, low, norm)
        h, l = split(fr_ref[0])
        frh[...] = h
        frl[...] = l
        piece_out[...] = piece_ref[0]

    update = product(split(fl_ref[0]), (frh[...], frl[...]), ((1,), (1,)))
    out_ref[...] = gauss_tile(xl_ref, high, low, norm) + d_ref[...] - update


def remaining_matrix(scalars, xg, factors, downdates):
    rows = downdates.shape[0]
    width = xg.shape[-1]
    per = TILE // width
    steps = PANEL // TILE
    spec = pltpu.PrefetchScalarGridSpec(
        num_scalar_prefetch=1,
        grid=(rows // TILE,),
        in_specs=[
            pl.BlockSpec((1, per, FEAT, width), lambda i, s: (i // steps, i % steps, 0, 0)),
            pl.BlockSpec((1, 8, FEAT, width), lambda i, s: (s[4], 0, 0, 0)),
            pl.BlockSpec((1, TILE, PANEL), lambda i, s: (i // steps, i % steps, 0)),
            pl.BlockSpec((1, PANEL, PANEL), lambda i, s: (s[5], 0, 0)),
            pl.BlockSpec((1, width, PANEL), lambda i, s: (s[6], s[7], 0)),
            pl.BlockSpec((TILE, PANEL), lambda i, s: (i, 0)),
        ],
        out_specs=(
            pl.BlockSpec((TILE, PANEL), lambda i, s: (i, 0)),
            pl.BlockSpec((width, PANEL), lambda i, s: (0, 0)),
        ),
        scratch_shapes=[
            pltpu.VMEM((KPAD, PANEL), BF16),
            pltpu.VMEM((KPAD, PANEL), BF16),
            pltpu.VMEM((1, PANEL), F32),
            pltpu.VMEM((PANEL, PANEL), BF16),
            pltpu.VMEM((PANEL, PANEL), BF16),
        ],
    )
    return pl.pallas_call(
        remaining_kernel,
        grid_spec=spec,
        out_shape=(
            jax.ShapeDtypeStruct((rows, PANEL), F32),
            jax.ShapeDtypeStruct((width, PANEL), F32),
        ),
        name="remaining",
    )(scalars, xg, xg, factors, factors, factors, downdates)


def spread_kernel(root, f_ref, g, rrow, rcol, rcore, srow, scol, score):
    p = place()
    near = neighbours(p)
    a = p["a"]
    size = PANEL // (2 * CHUNKS)
    y0, x0 = root % 4, root // 4
    d_row = (p["y"] - y0 + 4) % 4
    first_row = p["xl"] == x0
    is_root = first_row & (d_row == 0)
    d_col, first_col, diagonal = column_state(p)
    true = d_col >= 0
    entry_barrier(near)

    def rows(i):
        return pl.ds(pl.multiple_of(i * size, size), size)

    @pl.when(is_root)
    def _():
        def keep(i, carry):
            pltpu.make_async_copy(f_ref.at[rows(i)], g.at[a, rows(i)], rrow.at[i]).start()
            return carry

        lax.fori_loop(0, 2 * CHUNKS, keep, 0)

    def row_copies(m, e, part):
        i = m + part * CHUNKS
        here = g.at[a, rows(i)]
        flags = branch_flags(first_row, d_row, e, part)
        out = [
            (flag, remote(here, here, srow.at[n, 2 * e + part], rrow.at[i], near[way]))
            for n, (flag, way) in enumerate(zip(flags, ("yp", "ym", "xp")))
        ]
        out.append((true, remote(here, here, score.at[0], rcore.at[0], near["co"])))
        return out

    def column_copies(m, e, part, from_row):
        i = m + part * CHUNKS
        src = g.at[a, rows(i)] if from_row else g.at[2, rows(i)]
        dst = g.at[2, rows(i)]
        flags = branch_flags(true, 0 * d_col, e, part) if from_row else branch_flags(first_col, d_col, e, part)
        return [
            (flag, remote(src, dst, scol.at[n, 2 * e + part], rcol.at[i], near[way]))
            for n, (flag, way) in enumerate(zip(flags, ("zp", "zm", "xx")))
        ]

    def each(copies, act):
        for flag, copy in copies:
            @pl.when(flag)
            def _():
                act(copy)

    row_lag = {}
    col_lag = {}
    for e in range(4):
        for part in range(2):
            row_lag[e, part] = SKEW * hops(first_row, d_row, e, part)
            col_lag[e, part] = row_lag[e, part] + SKEW * hops(first_col, d_col, e, part)

    def turn(t, carry):
        for e in range(4):
            for part in range(2):
                m = t - row_lag[e, part]

                @pl.when((m >= 0) & (m < CHUNKS) & ((m + 256) % 4 == e))
                def _():
                    i = m + part * CHUNKS
                    here = g.at[a, rows(i)]
                    pltpu.make_async_copy(here, here, rrow.at[i]).wait()
                    each(row_copies(m, e, part), lambda copy: copy.start())

                    @pl.when(diagonal)
                    def _():
                        each(column_copies(m, e, part, True), lambda copy: copy.start())

                n = t - col_lag[e, part]

                @pl.when((n >= 0) & (n < CHUNKS) & ((n + 256) % 4 == e) & ~diagonal)
                def _():
                    i = n + part * CHUNKS
                    here = g.at[2, rows(i)]
                    pltpu.make_async_copy(here, here, rcol.at[i]).wait()
                    each(column_copies(n, e, part, False), lambda copy: copy.start())

        return carry

    lax.fori_loop(0, CHUNKS + 12 * SKEW, turn, 0)

    def whole(ref, sem):
        pltpu.make_async_copy(ref, ref, sem).wait()

    eighth = PANEL // 8
    for e in range(4):
        for part in range(2):
            along = branch_flags(first_row, d_row, e, part)
            at_root = branch_flags(true, 0 * d_col, e, part)
            below = branch_flags(first_col, d_col, e, part)
            for n in range(3):
                @pl.when(along[n])
                def _():
                    whole(g.at[a, pl.ds(0, eighth)], srow.at[n, 2 * e + part])

                @pl.when((diagonal & at_root[n]) | (~diagonal & below[n]))
                def _():
                    whole(g.at[a, pl.ds(0, eighth)], scol.at[n, 2 * e + part])

    whole(g.at[a], score.at[0])
    whole(g.at[1 - a], rcore.at[0])


def spread(root, half):
    dma = pltpu.SemaphoreType.DMA
    n = 2 * CHUNKS
    return pl.pallas_call(
        functools.partial(spread_kernel, root),
        out_shape=jax.ShapeDtypeStruct((3, PANEL, PANEL), F32),
        in_specs=[pl.BlockSpec(memory_space=pltpu.VMEM)],
        out_specs=pl.BlockSpec(memory_space=pl.ANY),
        scratch_shapes=[dma((n,)), dma((n,)), dma((1,)), dma((3, 8)), dma((3, 8)), dma((1,))],
        compiler_params=pltpu.CompilerParams(collective_id=1 + root, has_side_effects=True),
        name="spread" + str(root),
    )(half)


def shards(downdates, centers, diag_inverse, block_map, panel_index):
    row = lax.axis_index("row")
    col = lax.axis_index("col")
    core = col % 2
    diagonal = row == col // 2
    block_ids = jnp.arange(BLOCKS, dtype=jnp.int32)
    panel_block = jnp.sum(block_ids * (block_map == panel_index[0]).astype(jnp.int32))
    alive = jnp.sum(jnp.where(block_ids == 2 * row + core, block_map, 0)) > panel_index[0]
    base = jnp.where(diagonal, 0, 2)
    scalars = jnp.stack(
        [
            core,
            base + panel_block % 2,
            (panel_block % 2 == core).astype(jnp.int32),
            alive.astype(jnp.int32),
            base + core,
            jnp.where(diagonal, core, 2),
            col // 8,
            col % 8,
        ]
    ).astype(jnp.int32)
    xg, li, dx = gather(centers, diag_inverse, downdates)
    half = panel_factor(scalars, xg, li.reshape(PANEL, PANEL), downdates, dx)
    factors = lax.switch(panel_block // 2, [functools.partial(spread, root) for root in range(BLOCKS // 2)], half)
    remaining, piece = remaining_matrix(scalars, xg, factors, downdates)
    return piece, remaining


def solution(mesh):
    return jax.shard_map(
        shards,
        mesh=mesh,
        in_specs=(P("row", "col"), P(None, ("row", "col")), P("col", None), P(), P()),
        out_specs=(P(("row", "col"), None), P("row", "col")),
        check_vma=False,
    )
```

```python
import functools

import jax
import jax.numpy as jnp
from jax import lax
from jax.experimental import pallas as pl
from jax.experimental.pallas import tpu as pltpu
from jax.sharding import PartitionSpec as P

PANEL = 1024
FEAT = 440
KPAD = 512
BLOCKS = 16
MESH = pl.DeviceIdType.MESH
F32 = jnp.float32
BF16 = jnp.bfloat16
CHUNKS = 64
SKEW = 5
PIECES = 5
CENTER_SKEW = 4


def place():
    row = lax.axis_index("row")
    col = lax.axis_index("col")
    return dict(z=row // 2, xh=row % 2, xl=col // 8, y=(col // 2) % 4, a=col % 2)


def device(p, **changes):
    q = dict(p)
    q.update(changes)
    return (q["z"] * 2 + q["xh"], q["xl"] * 8 + q["y"] * 2 + q["a"])


def neighbours(p):
    return dict(
        yp=device(p, y=(p["y"] + 1) % 4),
        ym=device(p, y=(p["y"] + 3) % 4),
        xp=device(p, xl=1 - p["xl"]),
        zp=device(p, z=(p["z"] + 1) % 4),
        zm=device(p, z=(p["z"] + 3) % 4),
        xx=device(p, xh=1 - p["xh"]),
        co=device(p, a=1 - p["a"]),
    )


def entry_barrier(near):
    barrier = pltpu.get_barrier_semaphore()
    for where in near.values():
        pl.semaphore_signal(barrier, inc=1, device_id=where, device_id_type=MESH)
    pl.semaphore_wait(barrier, len(near))


def remote(src, dst, send, recv, where):
    return pltpu.make_async_remote_copy(
        src_ref=src, dst_ref=dst, send_sem=send, recv_sem=recv, device_id=where, device_id_type=MESH
    )


def branch_flags(first_ring, d, m, part):
    rel = (d - m + 16) % 4
    if part == 0:
        up = (first_ring & (d != 3)) | (~first_ring & (rel <= 1))
        down = ~first_ring & (rel == 0)
    else:
        up = ~first_ring & (rel == 0)
        down = (first_ring & (d != 1)) | (~first_ring & ((rel == 0) | (rel == 3)))
    across = first_ring & (rel == 0)
    return up, down, across


def hops(first_ring, d, e, part):
    rel = (d - e + 4) % 4
    near_e = e if part == 0 else (4 - e) % 4
    in_first = d if part == 0 else (4 - d) % 4
    return jnp.where(first_ring, in_first, near_e + 1 + jnp.minimum(rel, 4 - rel))


def column_state(p):
    k = p["xl"] * 4 + p["y"]
    d = (p["z"] - k // 2 + 4) % 4
    first = p["xh"] == k % 2
    diagonal = (p["z"] * 2 + p["xh"]) == k
    return d, first, diagonal


def gather_kernel(x_ref, l_ref, d_ref, xg, li, dx, own, rx, rl, rk, rc, sx, sl, sk, sc, sd):
    p = place()
    near = neighbours(p)
    a, y, xl = p["a"], p["y"], p["xl"]
    d, first, diagonal = column_state(p)
    entry_barrier(near)

    def slot(xl_, y_, a_):
        return xl_ * 8 + y_ * 2 + a_

    def at(table, s):
        return xg.at[s // 8, s % 8] if table == 0 else li.at[s]

    started = []

    def row_copy(table, s, way, src):
        src = at(table, s) if src is None else src
        sems, recv = (sx, rx) if table == 0 else (sl, rl)
        way_index = ("yp", "ym", "xp", "co").index(way)
        return remote(src, at(table, s), sems.at[way_index, s], recv.at[s], near[way])

    def send(table, s, way, src=None):
        row_copy(table, s, way, src).start()
        started.append((table, s, way, src))

    def arrived(table, s):
        recv = rx if table == 0 else rl
        copy = pltpu.make_async_copy(at(table, s), at(table, s), recv.at[s])
        copy.wait()

    mine = slot(xl, y, a)
    before, after, far = (y + 3) % 4, (y + 1) % 4, (y + 2) % 4

    def first_sends(table):
        src = x_ref if table == 0 else l_ref
        for way in ("yp", "ym", "xp", "co"):
            send(table, mine, way, src)
        keep = pltpu.make_async_copy(src, at(table, mine), own.at[table])
        keep.start()
        return keep

    half = PANEL
    swap = remote(d_ref.at[pl.ds((1 - a) * half, half)], dx, sd.at[0], sd.at[1], near["co"])
    swap.start()
    keep_x = first_sends(0)

    def row_steps(table):
        steps = []

        def step(s, *ways):
            def run():
                arrived(table, s)
                for way in ways:
                    send(table, s, way)

            steps.append(run)

        step(slot(1 - xl, y, a), "yp", "ym", "co")
        if table == 0:
            step(slot(xl, before, a), "yp", "co")
            step(slot(xl, after, a), "co")
        else:
            step(slot(xl, after, a), "ym", "co")
            step(slot(xl, before, a), "co")
        step(slot(1 - xl, before, a), "co")
        step(slot(1 - xl, after, a), "co")
        step(slot(xl, far, a), "xp", "co")
        step(slot(1 - xl, far, a), "co")
        return steps

    for run in row_steps(0):
        run()
    for xs in range(2):
        for ys in range(4):
            arrived(0, slot(xs, ys, 1 - a))
    keep_x.wait()

    chunks = 4 * PIECES
    tall = FEAT // PIECES
    true = d >= 0

    def piece(table, n, part):
        return xg.at[table, 2 * (n // PIECES) + part, pl.ds(pl.multiple_of((n % PIECES) * tall, 8), tall)]

    def column_copies(n, e, part, is_root):
        c = part * chunks + n
        src = piece(a, n, part) if is_root else piece(2 + a, n, part)
        flags = branch_flags(true, 0 * d, e, part) if is_root else branch_flags(first, d, e, part)
        return [
            (flag, remote(src, piece(2 + a, n, part), sk.at[index, 2 * e + part], rk.at[c], near[way]))
            for index, (flag, way) in enumerate(zip(flags, ("zp", "zm", "xx")))
        ]

    def core_copy(n, part):
        here = piece(2 + a, n, part)
        return remote(here, here, sc.at[0], rc.at[0], near["co"])

    def each(copies, act):
        for flag, copy in copies:
            @pl.when(flag)
            def _():
                act(copy)

    @pl.when(diagonal)
    def _():
        def issue(group, carry):
            for e in range(4):
                for part in range(2):
                    each(column_copies(4 * group + e, e, part, True), lambda copy: copy.start())
            return carry

        lax.fori_loop(0, PIECES, issue, 0)

    keep_l = first_sends(1)

    lag = {}
    for e in range(4):
        for part in range(2):
            lag[e, part] = CENTER_SKEW * hops(first, d, e, part)

    rest = row_steps(1)
    turns = chunks + 6 * CENTER_SKEW
    cuts = {turns // 5: rest[:3], 2 * turns // 5: rest[3:6], 3 * turns // 5: rest[6:]}

    def turn(t, carry):
        for cut, steps in cuts.items():
            @pl.when(t == cut)
            def _():
                for run in steps:
                    run()

        for e in range(4):
            for part in range(2):
                n = t - lag[e, part]

                @pl.when((n >= 0) & (n < chunks) & ((n + 256) % 4 == e) & ~diagonal)
                def _():
                    here = piece(2 + a, n, part)
                    pltpu.make_async_copy(here, here, rk.at[part * chunks + n]).wait()
                    each(column_copies(n, e, part, False), lambda copy: copy.start())
                    core_copy(n, part).start()

        return carry

    lax.fori_loop(0, turns, turn, 0)

    for xs in range(2):
        for ys in range(4):
            arrived(1, slot(xs, ys, 1 - a))
    keep_l.wait()
    swap.wait()

    def whole(ref, sem):
        pltpu.make_async_copy(ref, ref, sem).wait()

    for e in range(4):
        for part in range(2):
            at_root = branch_flags(true, 0 * d, e, part)
            below = branch_flags(first, d, e, part)
            for index in range(3):
                @pl.when((diagonal & at_root[index]) | (~diagonal & below[index]))
                def _():
                    whole(xg.at[2 + a, 0], sk.at[index, 2 * e + part])

    @pl.when(~diagonal)
    def _():
        whole(xg.at[2 + a], sc.at[0])
        whole(xg.at[3 - a], rc.at[0])

    for copy in started:
        row_copy(*copy).wait_send()


def gather(centers, inverse, downdates):
    dma = pltpu.SemaphoreType.DMA
    anywhere = pl.BlockSpec(memory_space=pl.ANY)
    vmem = pl.BlockSpec(memory_space=pltpu.VMEM)
    width = centers.shape[1]
    rows = inverse.shape[0]
    return pl.pallas_call(
        gather_kernel,
        out_shape=(
            jax.ShapeDtypeStruct((4, 8, FEAT, width), F32),
            jax.ShapeDtypeStruct((16, rows, PANEL), F32),
            jax.ShapeDtypeStruct((PANEL, PANEL), F32),
        ),
        in_specs=[vmem, vmem, anywhere],
        out_specs=(anywhere, anywhere, anywhere),
        scratch_shapes=[
            dma((2,)),
            dma((16,)),
            dma((16,)),
            dma((8 * PIECES,)),
            dma((1,)),
            dma((4, 16)),
            dma((4, 16)),
            dma((3, 8)),
            dma((1,)),
            dma((2,)),
        ],
        compiler_params=pltpu.CompilerParams(collective_id=0, has_side_effects=True),
        name="gather",
    )(centers, inverse, downdates)


def split(value):
    high = value.astype(BF16)
    low = (value - high.astype(F32)).astype(BF16)
    return high, low


def product(left, right, dims):
    dot = functools.partial(lax.dot_general, dimension_numbers=((dims), ((), ())), preferred_element_type=F32)
    (lh, ll), (rh, rl) = left, right
    return dot(lh, rh) + (dot(lh, rl) + dot(ll, rh))


def set_right(x_ref, high, low, norm):
    width = x_ref.shape[-1]
    for j in range(8):
        block = x_ref[0, j]
        norm[:, j * width : (j + 1) * width] = jnp.sum(block * block, axis=0, keepdims=True)
        block = jnp.concatenate([block, jnp.zeros((KPAD - FEAT, width), F32)], axis=0)
        h, l = split(block)
        high[:, j * width : (j + 1) * width] = h
        low[:, j * width : (j + 1) * width] = l


def gauss_tile(left_ref, high, low, norm):
    left = [left_ref[0, j] for j in range(left_ref.shape[1])]
    width = left[0].shape[1]
    zero = jnp.zeros((KPAD - FEAT, width), F32)
    left = jnp.concatenate([jnp.concatenate([block, zero], axis=0).T for block in left], axis=0)
    left_norm = jnp.sum(left * left, axis=1, keepdims=True)
    cross = product(split(left), (high[...], low[...]), ((1,), (0,)))
    return jnp.exp(-(0.5 / FEAT) * (left_norm + norm[...] - 2.0 * cross))


def factor_kernel(s_ref, xl_ref, xr_ref, li_ref, d_ref, dx_ref, out_ref, high, low, norm, lih, lil):
    @pl.when(pl.program_id(0) == 0)
    def _():
        set_right(xr_ref, high, low, norm)
        h, l = split(li_ref[...])
        lih[...] = h
        lil[...] = l

    raw = gauss_tile(xl_ref, high, low, norm) + jnp.where(s_ref[2] == 1, d_ref[...], dx_ref[...])
    rh, rl = split(raw)
    for start in range(0, PANEL, TILE):
        stop = start + TILE
        block = (lih[start:stop, :stop], lil[start:stop, :stop])
        result = product((rh[:, :stop], rl[:, :stop]), block, ((1,), (1,)))
        out_ref[:, start:stop] = jnp.where(s_ref[3] == 1, result, 0.0)


TILE = 256


def panel_factor(scalars, xg, li, downdates, dx):
    per = TILE // xg.shape[-1]
    spec = pltpu.PrefetchScalarGridSpec(
        num_scalar_prefetch=1,
        grid=(PANEL // TILE,),
        in_specs=[
            pl.BlockSpec((1, per, FEAT, xg.shape[-1]), lambda i, s: (s[0], i, 0, 0)),
            pl.BlockSpec((1, 8, FEAT, xg.shape[-1]), lambda i, s: (s[1], 0, 0, 0)),
            pl.BlockSpec((PANEL, PANEL), lambda i, s: (0, 0)),
            pl.BlockSpec((TILE, PANEL), lambda i, s: (s[0] * (PANEL // TILE) + i, 0)),
            pl.BlockSpec((TILE, PANEL), lambda i, s: (i, 0)),
        ],
        out_specs=pl.BlockSpec((TILE, PANEL), lambda i, s: (i, 0)),
        scratch_shapes=[
            pltpu.VMEM((KPAD, PANEL), BF16),
            pltpu.VMEM((KPAD, PANEL), BF16),
            pltpu.VMEM((1, PANEL), F32),
            pltpu.VMEM((PANEL, PANEL), BF16),
            pltpu.VMEM((PANEL, PANEL), BF16),
        ],
    )
    return pl.pallas_call(
        factor_kernel, grid_spec=spec, out_shape=jax.ShapeDtypeStruct((PANEL, PANEL), F32), name="factor"
    )(scalars, xg, xg, li, downdates, dx)


def remaining_kernel(s_ref, xl_ref, xr_ref, fl_ref, fr_ref, piece_ref, d_ref, out_ref, piece_out, high, low, norm, frh, frl):
    @pl.when(pl.program_id(0) == 0)
    def _():
        set_right(xr_ref, high, low, norm)
        h, l = split(fr_ref[0])
        frh[...] = h
        frl[...] = l
        piece_out[...] = piece_ref[0]

    update = product(split(fl_ref[0]), (frh[...], frl[...]), ((1,), (1,)))
    out_ref[...] = gauss_tile(xl_ref, high, low, norm) + d_ref[...] - update


def remaining_matrix(scalars, xg, factors, downdates):
    rows = downdates.shape[0]
    width = xg.shape[-1]
    per = TILE // width
    steps = PANEL // TILE
    spec = pltpu.PrefetchScalarGridSpec(
        num_scalar_prefetch=1,
        grid=(rows // TILE,),
        in_specs=[
            pl.BlockSpec((1, per, FEAT, width), lambda i, s: (i // steps, i % steps, 0, 0)),
            pl.BlockSpec((1, 8, FEAT, width), lambda i, s: (s[4], 0, 0, 0)),
            pl.BlockSpec((1, TILE, PANEL), lambda i, s: (i // steps, i % steps, 0)),
            pl.BlockSpec((1, PANEL, PANEL), lambda i, s: (s[5], 0, 0)),
            pl.BlockSpec((1, width, PANEL), lambda i, s: (s[6], s[7], 0)),
            pl.BlockSpec((TILE, PANEL), lambda i, s: (i, 0)),
        ],
        out_specs=(
            pl.BlockSpec((TILE, PANEL), lambda i, s: (i, 0)),
            pl.BlockSpec((width, PANEL), lambda i, s: (0, 0)),
        ),
        scratch_shapes=[
            pltpu.VMEM((KPAD, PANEL), BF16),
            pltpu.VMEM((KPAD, PANEL), BF16),
            pltpu.VMEM((1, PANEL), F32),
            pltpu.VMEM((PANEL, PANEL), BF16),
            pltpu.VMEM((PANEL, PANEL), BF16),
        ],
    )
    return pl.pallas_call(
        remaining_kernel,
        grid_spec=spec,
        out_shape=(
            jax.ShapeDtypeStruct((rows, PANEL), F32),
            jax.ShapeDtypeStruct((width, PANEL), F32),
        ),
        name="remaining",
    )(scalars, xg, xg, factors, factors, factors, downdates)


def spread_kernel(root, f_ref, g, rrow, rcol, rcore, srow, scol, score):
    p = place()
    near = neighbours(p)
    a = p["a"]
    size = PANEL // (2 * CHUNKS)
    y0, x0 = root % 4, root // 4
    d_row = (p["y"] - y0 + 4) % 4
    first_row = p["xl"] == x0
    is_root = first_row & (d_row == 0)
    d_col, first_col, diagonal = column_state(p)
    true = d_col >= 0
    entry_barrier(near)

    def rows(i):
        return pl.ds(pl.multiple_of(i * size, size), size)

    @pl.when(is_root)
    def _():
        def keep(i, carry):
            pltpu.make_async_copy(f_ref.at[rows(i)], g.at[a, rows(i)], rrow.at[i]).start()
            return carry

        lax.fori_loop(0, 2 * CHUNKS, keep, 0)

    def row_copies(m, e, part):
        i = m + part * CHUNKS
        here = g.at[a, rows(i)]
        flags = branch_flags(first_row, d_row, e, part)
        out = [
            (flag, remote(here, here, srow.at[n, 2 * e + part], rrow.at[i], near[way]))
            for n, (flag, way) in enumerate(zip(flags, ("yp", "ym", "xp")))
        ]
        out.append((true, remote(here, here, score.at[0], rcore.at[0], near["co"])))
        return out

    def column_copies(m, e, part, from_row):
        i = m + part * CHUNKS
        src = g.at[a, rows(i)] if from_row else g.at[2, rows(i)]
        dst = g.at[2, rows(i)]
        flags = branch_flags(true, 0 * d_col, e, part) if from_row else branch_flags(first_col, d_col, e, part)
        return [
            (flag, remote(src, dst, scol.at[n, 2 * e + part], rcol.at[i], near[way]))
            for n, (flag, way) in enumerate(zip(flags, ("zp", "zm", "xx")))
        ]

    def each(copies, act):
        for flag, copy in copies:
            @pl.when(flag)
            def _():
                act(copy)

    row_lag = {}
    col_lag = {}
    for e in range(4):
        for part in range(2):
            row_lag[e, part] = SKEW * hops(first_row, d_row, e, part)
            col_lag[e, part] = row_lag[e, part] + SKEW * hops(first_col, d_col, e, part)

    def turn(t, carry):
        for e in range(4):
            for part in range(2):
                m = t - row_lag[e, part]

                @pl.when((m >= 0) & (m < CHUNKS) & ((m + 256) % 4 == e))
                def _():
                    i = m + part * CHUNKS
                    here = g.at[a, rows(i)]
                    pltpu.make_async_copy(here, here, rrow.at[i]).wait()
                    each(row_copies(m, e, part), lambda copy: copy.start())

                    @pl.when(diagonal)
                    def _():
                        each(column_copies(m, e, part, True), lambda copy: copy.start())

                n = t - col_lag[e, part]

                @pl.when((n >= 0) & (n < CHUNKS) & ((n + 256) % 4 == e) & ~diagonal)
                def _():
                    i = n + part * CHUNKS
                    here = g.at[2, rows(i)]
                    pltpu.make_async_copy(here, here, rcol.at[i]).wait()
                    each(column_copies(n, e, part, False), lambda copy: copy.start())

        return carry

    lax.fori_loop(0, CHUNKS + 12 * SKEW, turn, 0)

    def whole(ref, sem):
        pltpu.make_async_copy(ref, ref, sem).wait()

    eighth = PANEL // 8
    for e in range(4):
        for part in range(2):
            along = branch_flags(first_row, d_row, e, part)
            at_root = branch_flags(true, 0 * d_col, e, part)
            below = branch_flags(first_col, d_col, e, part)
            for n in range(3):
                @pl.when(along[n])
                def _():
                    whole(g.at[a, pl.ds(0, eighth)], srow.at[n, 2 * e + part])

                @pl.when((diagonal & at_root[n]) | (~diagonal & below[n]))
                def _():
                    whole(g.at[a, pl.ds(0, eighth)], scol.at[n, 2 * e + part])

    whole(g.at[a], score.at[0])
    whole(g.at[1 - a], rcore.at[0])


def spread(root, half):
    dma = pltpu.SemaphoreType.DMA
    n = 2 * CHUNKS
    return pl.pallas_call(
        functools.partial(spread_kernel, root),
        out_shape=jax.ShapeDtypeStruct((3, PANEL, PANEL), F32),
        in_specs=[pl.BlockSpec(memory_space=pltpu.VMEM)],
        out_specs=pl.BlockSpec(memory_space=pl.ANY),
        scratch_shapes=[dma((n,)), dma((n,)), dma((1,)), dma((3, 8)), dma((3, 8)), dma((1,))],
        compiler_params=pltpu.CompilerParams(collective_id=1 + root, has_side_effects=True),
        name="spread" + str(root),
    )(half)


def shards(downdates, centers, diag_inverse, block_map, panel_index):
    row = lax.axis_index("row")
    col = lax.axis_index("col")
    core = col % 2
    diagonal = row == col // 2
    block_ids = jnp.arange(BLOCKS, dtype=jnp.int32)
    panel_block = jnp.sum(block_ids * (block_map == panel_index[0]).astype(jnp.int32))
    alive = jnp.sum(jnp.where(block_ids == 2 * row + core, block_map, 0)) > panel_index[0]
    base = jnp.where(diagonal, 0, 2)
    scalars = jnp.stack(
        [
            core,
            base + panel_block % 2,
            (panel_block % 2 == core).astype(jnp.int32),
            alive.astype(jnp.int32),
            base + core,
            jnp.where(diagonal, core, 2),
            col // 8,
            col % 8,
        ]
    ).astype(jnp.int32)
    xg, li, dx = gather(centers, diag_inverse, downdates)
    half = panel_factor(scalars, xg, li.reshape(PANEL, PANEL), downdates, dx)
    factors = lax.switch(panel_block // 2, [functools.partial(spread, root) for root in range(BLOCKS // 2)], half)
    remaining, piece = remaining_matrix(scalars, xg, factors, downdates)
    return piece, remaining


def solution(mesh):
    return jax.shard_map(
        shards,
        mesh=mesh,
        in_specs=(P("row", "col"), P(None, ("row", "col")), P("col", None), P(), P()),
        out_specs=(P(("row", "col"), None), P("row", "col")),
        check_vma=False,
    )
```
